512 devices in a mesh: gx: 16 (over x_lo, z), gy: 4 (over x_hi, core), gz: 8 (over y).
Axes of the slice: x: 4 (x_hi: 2, x_lo: 2; x = x_hi * 2 + x_lo), y: 8, z: 8, core: 2. Of those that a mesh axis runs over, the one named last changes fastest.
Arguments:
- gas: float32 [6, 128, 32, 1024], P(None, 'gx', 'gy', 'gz'), may hold values from -1.5 to 6, as said below
- parcels: float32 [32768, 5, 128], P(('gx', 'gy', 'gz')), may hold values from -1 to 2, as said below
- home_cell_index: int32 [32768, 128], P(('gx', 'gy', 'gz')), may hold values from 0 to 8191
- order: int32 [512, 64], P(('gx', 'gy', 'gz')), may hold values from 0 to 63, each once within a row
- counts: int32 [512, 3], P(('gx', 'gy', 'gz')), may hold values from 0 to 32, as said below
Outputs:
- gas_out: float32 [6, 128, 32, 1024], P(None, 'gx', 'gy', 'gz')
- moved_parcels: float32 [32768, 5, 128], P(('gx', 'gy', 'gz'))
The draws below stay inside these ranges and needn't reach their ends.
Inputs may be any that keep to these rules, and one draw needn't show every extreme that they name: `gas`: gas density lies in 0.8 to 1.6, pressure in 0.8 to 1.6, velocities within 0.8, vapour fraction in 0.05 to 0.3. `parcels`: parcel masses lie in 0.2 to 2, temperatures in 0.3 to 1.2, velocities in -1 to 1.5. `counts`: kept is at most 32, forward and back each at most 16; each bound is reached in every draw.
All inputs are finite; a program needn't handle non-finite values.
Results may differ from the reference program's by a relative error of at most 0.00002.
Values sent between devices are 32-bit elements; how exact they have to be, the bound alone decides.
No kernel may reach another device: no remote copies, remote signals or barrier semaphores. Data moves between devices by JAX's collectives and lax.ppermute only.
A program may use at most 64 MiB of HBM per device.

```python
import jax
import jax.numpy as jnp
from jax import lax

AXIAL_CELLS = 8
CROSSWISE_CELLS = 8
LATERAL_CELLS = 128
BLK_DEV = 64
NX = 128
NY = 32
NZ = 1024
PACKET_ROOM = 32768
N_GX = 16
N_GY = 4
N_GZ = 8
DEVICES = 512


GAMMA = 1.4


def draw_gas(key, part):
    chance_generator_inputs = jax.random.split(jax.random.fold_in(key, 5), 5)
    grid_shape = (NX, NY, NZ)
    density = jax.random.uniform(chance_generator_inputs[0], grid_shape, jnp.float32, 0.8, 1.6)
    spray_drop_momentum_tendency = jax.random.uniform(chance_generator_inputs[1], (3,) + grid_shape, jnp.float32, -0.5, 0.5)
    pressure = jax.random.uniform(chance_generator_inputs[2], grid_shape, jnp.float32, 0.8, 1.6)
    fraction = jax.random.uniform(chance_generator_inputs[3], grid_shape, jnp.float32, 0.05, 0.3)
    momentum = density[None] * spray_drop_momentum_tendency
    energy = pressure / (GAMMA - 1.0) + 0.5 * density * jnp.sum(spray_drop_momentum_tendency * spray_drop_momentum_tendency, axis=0)
    return jnp.concatenate([density[None], momentum, energy[None], (density * fraction)[None]], axis=0).astype(jnp.float32)


def draw_parcels(key, part):
    chance_generator_inputs = jax.random.split(jax.random.fold_in(key, 7), 3)
    spray_drop_momentum_tendency = jax.random.uniform(chance_generator_inputs[0], (PACKET_ROOM, 3, 128), jnp.float32, -1.0, 1.0)
    spray_drop_ln_multiplicity = jax.random.uniform(chance_generator_inputs[1], (PACKET_ROOM, 1, 128), jnp.float32, jnp.log(0.2), jnp.log(2.0))
    spray_drop_warmth_measure = jax.random.uniform(chance_generator_inputs[2], (PACKET_ROOM, 1, 128), jnp.float32, 0.3, 1.2)
    return jnp.concatenate([spray_drop_momentum_tendency, jnp.exp(spray_drop_ln_multiplicity), spray_drop_warmth_measure], axis=1).astype(jnp.float32)


def draw_counts(key, part):
    chance_generator_inputs = jax.random.split(jax.random.fold_in(key, 17), 3)
    dev_ids = jnp.arange(DEVICES, dtype=jnp.int32)
    slab_dev = dev_ids // (N_GY * N_GZ)
    half_cap = BLK_DEV // 2
    move_cap = BLK_DEV // 4
    limit = half_cap * (slab_dev + 1) // N_GX
    kept = jax.random.randint(chance_generator_inputs[0], (DEVICES,), 0, limit + 1)
    kept = jnp.where(slab_dev == N_GX - 1, half_cap, kept)
    forward = jax.random.randint(chance_generator_inputs[1], (DEVICES,), 0, move_cap + 1)
    forward = jnp.where(dev_ids == 0, move_cap, forward)
    backward = jax.random.randint(chance_generator_inputs[2], (DEVICES,), 0, move_cap + 1)
    backward = jnp.where(dev_ids == N_GY * N_GZ, move_cap, backward)
    return jnp.stack([kept, forward, backward], axis=1).astype(jnp.int32)


def set_ends(array, key, least, top_value):
    longest = array.shape.index(max(array.shape))
    spots = []
    for shift in (0, 1):
        where = [jax.random.randint(jax.random.fold_in(key, axis), (), 0, length) for axis, length in enumerate(array.shape)]
        where[longest] = (where[longest] + shift) % array.shape[longest]
        spots.append(tuple(where))
    return array.at[spots[0]].set(least).at[spots[1]].set(top_value)


def setup_inputs(seed: int = 0) -> dict:
    key_list = jax.random.split(jax.random.key(seed), 6)
    gas = draw_gas(jax.random.fold_in(key_list[5], 71), 0)
    parcels = draw_parcels(jax.random.fold_in(key_list[5], 71), 0)
    home_cell_index = set_ends(jax.random.randint(key_list[2], (PACKET_ROOM, 128), 0, AXIAL_CELLS * CROSSWISE_CELLS * LATERAL_CELLS), jax.random.fold_in(key_list[2], 1), 0, (AXIAL_CELLS * CROSSWISE_CELLS * LATERAL_CELLS) - 1).astype(jnp.int32)
    order = jax.vmap(lambda own: jax.random.permutation(own, BLK_DEV))(jax.random.split(key_list[3], DEVICES)).reshape((DEVICES, BLK_DEV)).astype(jnp.int32)
    counts = draw_counts(jax.random.fold_in(key_list[5], 71), 0)
    return {"gas": gas, "parcels": parcels, "home_cell_index": home_cell_index, "order": order, "counts": counts}


GAMMA = 1.4
TIME_STEP = 0.1
RATE = 3.0
ACTIVATION = 2.0
HEAT = 5.0
DRAG_RELAX_TIME = 0.4
HEATING_RELAX = 0.6
EVAP_RATE = 1.5
LIQUID_HEAT = 2.0

def pressure_of(gas_state):
    motion_energy = gas_state[1] * gas_state[1] + gas_state[2] * gas_state[2] + gas_state[3] * gas_state[3]
    return (GAMMA - 1.0) * (gas_state[4] - 0.5 * motion_energy / gas_state[0])

def directional(column, direction):
    density = column[0]
    speed_along = column[1 + direction] / density
    pressure = pressure_of(column)
    pieces = [column[1 + direction], column[1] * speed_along, column[2] * speed_along, column[3] * speed_along, (column[4] + pressure) * speed_along, column[5] * speed_along]
    pieces[1 + direction] = pieces[1 + direction] + pressure
    return (jnp.stack(pieces), jnp.abs(speed_along) + jnp.sqrt(GAMMA * pressure / density))

def tendency(padded):
    interior = padded[:, 1:-1, 1:-1, 1:-1]
    result = jnp.zeros_like(interior)
    for direction in range(3):
        window = [slice(None), slice(1, -1), slice(1, -1), slice(1, -1)]
        window[direction + 1] = slice(None)
        column = padded[tuple(window)]
        fluxes, speeds = directional(column, direction)
        array_dim = direction + 1
        length = column.shape[array_dim]
        lower_flux = lax.slice_in_dim(fluxes, 0, length - 1, axis=array_dim)
        upper_flux = lax.slice_in_dim(fluxes, 1, length, axis=array_dim)
        lower_speed = lax.slice_in_dim(speeds, 0, length - 1, axis=direction)
        upper_speed = lax.slice_in_dim(speeds, 1, length, axis=direction)
        left_neighbor_fields = lax.slice_in_dim(column, 0, length - 1, axis=array_dim)
        upper_state = lax.slice_in_dim(column, 1, length, axis=array_dim)
        face_flux = 0.5 * (lower_flux + upper_flux) - 0.5 * jnp.maximum(lower_speed, upper_speed)[None] * (upper_state - left_neighbor_fields)
        result = result - (lax.slice_in_dim(face_flux, 1, length - 1, axis=array_dim) - lax.slice_in_dim(face_flux, 0, length - 2, axis=array_dim))
    burned = RATE * interior[5] * jnp.exp(-ACTIVATION * interior[0] / pressure_of(interior))
    result = result.at[4].add(HEAT * burned)
    result = result.at[5].add(-burned)
    return result

def parcel_update(parcels, transported):
    density = transported[0]
    gas_velocity = transported[1:4] / density
    gas_temp = pressure_of(transported) / density
    vapour = transported[5] / density
    drop_velocity = jnp.moveaxis(parcels[:, 0:3], 1, 0)
    drop_mass = parcels[:, 3]
    drop_temp = parcels[:, 4]
    root_mass = jnp.sqrt(drop_mass)
    new_mass = drop_mass * jnp.exp(-TIME_STEP * EVAP_RATE * gas_temp / (root_mass * (1.0 + vapour * vapour)))
    new_velocity = gas_velocity + (drop_velocity - gas_velocity) * jnp.exp(-TIME_STEP / (DRAG_RELAX_TIME * root_mass))
    new_temp = gas_temp + (drop_temp - gas_temp) * jnp.exp(-TIME_STEP / (HEATING_RELAX * root_mass))
    mass_source = drop_mass - new_mass
    momentum_source = drop_mass * drop_velocity - new_mass * new_velocity
    energy_source = 0.5 * (drop_mass * lax.optimization_barrier(jnp.sum(drop_velocity * drop_velocity, axis=0)) - new_mass * lax.optimization_barrier(jnp.sum(new_velocity * new_velocity, axis=0))) + LIQUID_HEAT * (drop_mass * drop_temp - new_mass * new_temp)
    sources = jnp.stack([mass_source, momentum_source[0], momentum_source[1], momentum_source[2], energy_source, mass_source])
    updated = jnp.stack([new_velocity[0], new_velocity[1], new_velocity[2], new_mass, new_temp], axis=1)
    return (updated, sources)

def pad_edges(field):
    return jnp.pad(field, ((0, 0), (1, 1), (1, 1), (1, 1)), mode='edge')

def reference(gas, parcels, home_cell_index, order, counts):
    section_one = gas + TIME_STEP * tendency(pad_edges(gas))
    stepped = 0.5 * gas + 0.5 * (section_one + TIME_STEP * tendency(pad_edges(section_one)))
    raveled_vapour_state = stepped.reshape(6, -1)
    group_numbers = jnp.arange(PACKET_ROOM, dtype=jnp.int32)
    owner = group_numbers // BLK_DEV
    slab_x = owner // (N_GY * N_GZ)
    block_slab_second = owner // N_GZ % N_GY
    slab_z = owner % N_GZ
    local_x = home_cell_index // (CROSSWISE_CELLS * LATERAL_CELLS)
    local_y = home_cell_index // LATERAL_CELLS % CROSSWISE_CELLS
    local_z = home_cell_index % LATERAL_CELLS
    domainwide_cell_number = ((slab_x[:, None] * AXIAL_CELLS + local_x) * NY + block_slab_second[:, None] * CROSSWISE_CELLS + local_y) * NZ + slab_z[:, None] * LATERAL_CELLS + local_z
    domainwide_cell_number = domainwide_cell_number.astype(jnp.int32)
    dev_ids = jnp.arange(DEVICES, dtype=jnp.int32)
    slot_ids = jnp.arange(BLK_DEV, dtype=jnp.int32)
    positions = jnp.zeros((DEVICES, BLK_DEV), jnp.int32).at[dev_ids[:, None], order].set(jnp.broadcast_to(slot_ids[None, :], (DEVICES, BLK_DEV)))
    kept = counts[:, 0]
    forward = counts[:, 1]
    backward = counts[:, 2]
    live_total = kept + forward + backward
    live = (positions.reshape(-1) < live_total[owner]).astype(jnp.float32)
    transported = raveled_vapour_state[:, domainwide_cell_number.reshape(-1)].reshape(6, PACKET_ROOM, 128)
    updated, sources = parcel_update(parcels, transported)
    sources = sources * live[None, :, None]
    gas_out = raveled_vapour_state.at[:, domainwide_cell_number.reshape(-1)].add(sources.reshape(6, -1)).reshape(6, NX, NY, NZ)
    stride = N_GY * N_GZ
    slab_dev = dev_ids // stride
    has_lower = slab_dev > 0
    has_upper = slab_dev < N_GX - 1
    lower_dev = jnp.where(has_lower, dev_ids - stride, dev_ids)
    upper_dev = jnp.where(has_upper, dev_ids + stride, dev_ids)
    from_lower = jnp.where(has_lower, forward[lower_dev], 0)
    from_upper = jnp.where(has_upper, backward[upper_dev], 0)
    slot_grid = slot_ids[None, :]
    own_count = kept[:, None]
    lower_count = from_lower[:, None]
    upper_count = from_upper[:, None]
    in_own = slot_grid < own_count
    in_lower = (slot_grid >= own_count) & (slot_grid < own_count + lower_count)
    in_upper = (slot_grid >= own_count + lower_count) & (slot_grid < own_count + lower_count + upper_count)
    source_dev = jnp.where(in_own, dev_ids[:, None], jnp.where(in_lower, lower_dev[:, None], upper_dev[:, None]))
    source_pos = jnp.where(in_own, slot_grid, jnp.where(in_lower, kept[lower_dev][:, None] + slot_grid - own_count, kept[upper_dev][:, None] + forward[upper_dev][:, None] + slot_grid - own_count - lower_count))
    source_pos = jnp.clip(source_pos, 0, BLK_DEV - 1).astype(jnp.int32)
    valid = (in_own | in_lower | in_upper).reshape(-1)
    source_slot = order[source_dev, source_pos]
    source_block = (source_dev * BLK_DEV + source_slot).reshape(-1).astype(jnp.int32)
    moved_parcels = jnp.where(valid[:, None, None], updated[source_block], 0.0)
    return (gas_out, moved_parcels)
```

```python
import jax
import jax.numpy as jnp
from jax import lax
from jax.experimental import pallas as pl
from jax.experimental.pallas import tpu as pltpu
from jax.sharding import PartitionSpec as P

GAMMA = 1.4
TIME_STEP = 0.1
RATE = 3.0
ACTIVATION = 2.0
HEAT = 5.0
DRAG_RELAX_TIME = 0.4
HEATING_RELAX = 0.6
EVAP_RATE = 1.5
LIQUID_HEAT = 2.0

F32 = jnp.float32
BF16 = jnp.bfloat16
INTERPRET = False


def shifted(block, axis, step):
    count = lax.axis_size(axis)
    return lax.ppermute(block, axis, [(i, i + step) for i in range(count) if 0 <= i + step < count])


def ends(axis):
    at = lax.axis_index(axis)
    return at == 0, at == lax.axis_size(axis) - 1


def call(kernel, outs, **kwargs):
    return pl.pallas_call(
        kernel,
        out_shape=[jax.ShapeDtypeStruct(shape, F32) for shape in outs],
        interpret=INTERPRET,
        **kwargs,
    )


def sublane(shape):
    return lax.broadcasted_iota(jnp.int32, shape, len(shape) - 2)


def lane(shape):
    return lax.broadcasted_iota(jnp.int32, shape, len(shape) - 1)


def turn(v, shift, axis):
    size = v.shape[axis]
    shift %= size
    return v if shift == 0 else pltpu.roll(v, shift, axis)


def pack_y(gas, xlo, xhi, rows, low_pay, high_pay):
    first, last = ends("gx")
    sub = sublane((8, 128))
    for c in range(6):
        line = []
        for i in range(12):
            if i < 2:
                line.append(jnp.where(first, gas[c, 0], xlo[c, i]))
                rows[c, i] = line[-1]
            elif i < 10:
                line.append(gas[c, i - 2])
            else:
                line.append(jnp.where(last, gas[c, 7], xhi[c, i - 10]))
                rows[c, i - 8] = line[-1]
        for g in range(3):
            low = line[4 * g]
            high = turn(line[4 * g], 2, 0)
            for k in range(1, 4):
                here = (sub >= 2 * k) & (sub < 2 * k + 2)
                low = jnp.where(here, turn(line[4 * g + k], 2 * k, 0), low)
                high = jnp.where(here, turn(line[4 * g + k], 2 * k + 2, 0), high)
            low_pay[c, g] = low
            high_pay[c, g] = high


def pack_z(gas, rows, ylo, yhi, box, pay):
    first, last = ends("gy")
    sub = sublane((8, 128))
    group = lane((16, 128)) // 8
    for c in range(6):
        packed = None
        for i in range(12):
            if 2 <= i < 10:
                mid = gas[c, i - 2]
            else:
                mid = rows[c, i if i < 2 else i - 8]
            g, k = i // 4, i % 4
            below = turn(ylo[c, g], 6 - 2 * k, 0)
            above = turn(yhi[c, g], -2 * k, 0)
            below = jnp.where(first, jnp.broadcast_to(mid[0:1], (8, 128)), below)
            above = jnp.where(last, jnp.broadcast_to(mid[7:8], (8, 128)), above)
            line = jnp.concatenate([mid, jnp.where(sub < 4, above, below)], axis=0)
            box[c, i] = line
            moved = turn(line, 8 * i + 2, 1)
            packed = moved if packed is None else jnp.where(group == i, moved, packed)
        pay[c] = packed


def primitives(state):
    r, m1, m2, m3, e, _ = state
    inv = 1.0 / r
    u = (m1 * inv, m2 * inv, m3 * inv)
    p = (GAMMA - 1.0) * (e - 0.5 * (m1 * u[0] + m2 * u[1] + m3 * u[2]))
    return u, p, jnp.sqrt(GAMMA * p * inv)


def along(state, prim, k):
    u, p, sound = prim
    uk = u[k]
    flux = [state[1 + k], state[1] * uk, state[2] * uk, state[3] * uk, (state[4] + p) * uk, state[5] * uk]
    flux[1 + k] = flux[1 + k] + p
    return flux, jnp.abs(uk) + sound, state


def face(lower, upper):
    speed = jnp.maximum(lower[1], upper[1])
    return [
        (fa + fb) - speed * (b - a)
        for fa, fb, a, b in zip(lower[0], upper[0], lower[2], upper[2], strict=True)
    ]


def over(part, move):
    flux, speed, state = part
    return [move(f) for f in flux], move(speed), [move(v) for v in state]


def advanced(state, prim, total):
    burned = RATE * state[5] * jnp.exp(-ACTIVATION * state[0] / prim[1])
    out = [v - (0.5 * TIME_STEP) * t for v, t in zip(state, total, strict=True)]
    out[4] = out[4] + (TIME_STEP * HEAT) * burned
    out[5] = out[5] - TIME_STEP * burned
    return out


def cyclic_net(state, prim, k, distance, axis):
    part = along(state, prim, k)
    faces = face(part, over(part, lambda v: turn(v, -distance, axis)))
    return faces, [f - turn(f, distance, axis) for f in faces]


def side_state(own, below, above, first, last):
    at = lane((16, 128)) % 8
    low = jnp.where(at < 2, jnp.where(first, jnp.where(at == 0, turn(own, -2, 1), turn(own, -1, 1)), below), own)
    high = jnp.where(at < 2, own, jnp.where(last, jnp.where(at == 2, turn(own, 1, 1), turn(own, 2, 1)), above))
    return jnp.where(at < 4, low, turn(high, 4, 1))


def side_inflow(faces):
    at = lane((16, 128)) % 8
    return [jnp.where(at == 0, turn(f, -5, 1), -f) for f in faces]


def closed_net(part, inflow, i):
    at = lane(part[1].shape)
    faces = face(part, over(part, lambda v: turn(v, -1, 1)))
    net = []
    for f, s in zip(faces, inflow, strict=True):
        f = jnp.where(at == 127, 0.0, f)
        outer = turn(s[: f.shape[0]], 127 - 8 * i, 1)
        net.append(f - turn(f, 1, 1) + jnp.where((at == 0) | (at == 127), outer, 0.0))
    return net


def gas_step(box, own, below, above, stepped, ahead):
    first_x, last_x = ends("gx")
    first_y, last_y = ends("gy")
    first_z, last_z = ends("gz")
    sub = sublane((16, 128))
    at = lane((16, 128)) % 8
    group = lane((16, 128)) // 8

    def clamp_y(v):
        v = jnp.where(first_y & (sub == 15), jnp.broadcast_to(v[0:1], v.shape), v)
        return jnp.where(last_y & (sub == 8), jnp.broadcast_to(v[7:8], v.shape), v)

    def clamp_x_z(v):
        v = jnp.where(first_x & (group == 1), turn(v, -8, 1), v)
        v = jnp.where(last_x & (group == 10), turn(v, 8, 1), v)
        v = jnp.where(first_z & (at == 1), turn(v, -1, 1), v)
        return jnp.where(last_z & (at == 6), turn(v, 1, 1), v)

    side = [side_state(own[c], below[c], above[c], first_z, last_z) for c in range(6)]
    prim = primitives(side)
    faces, net_z = cyclic_net(side, prim, 2, 1, 1)
    inflow_one = side_inflow(faces)
    _, net_x = cyclic_net(side, prim, 0, 8, 1)
    _, net_y = cyclic_net(side, prim, 1, 1, 0)
    side = advanced(side, prim, [x + y + z for x, y, z in zip(net_x, net_y, net_z, strict=True)])
    side = [clamp_y(clamp_x_z(v)) for v in side]
    inflow_two = side_inflow(cyclic_net(side, primitives(side), 2, 1, 1)[0])

    state = [box[c, 0] for c in range(6)]
    part = along(state, primitives(state), 0)
    state = [box[c, 1] for c in range(6)]
    prim = primitives(state)
    next_part = along(state, prim, 0)
    faces = face(part, next_part)
    for i in range(1, 11):
        part = next_part
        next_state = [box[c, i + 1] for c in range(6)]
        next_prim = primitives(next_state)
        next_part = along(next_state, next_prim, 0)
        next_faces = face(part, next_part)
        _, net_y = cyclic_net(state, prim, 1, 1, 0)
        net_z = closed_net(along(state, prim, 2), inflow_one, i)
        total = [b - a + y + z for a, b, y, z in zip(faces, next_faces, net_y, net_z, strict=True)]
        for c, v in enumerate(advanced(state, prim, total)):
            ahead[c, i] = clamp_y(v)
        state, prim, faces = next_state, next_prim, next_faces

    def row(i):
        v = [ahead[c, i] for c in range(6)]
        if i == 1:
            v = [jnp.where(first_x, ahead[c, 2], v[c]) for c in range(6)]
        if i == 10:
            v = [jnp.where(last_x, ahead[c, 9], v[c]) for c in range(6)]
        return v

    def inner(values):
        return [v[:8] for v in values]

    def inner_prim(prim):
        return inner(prim[0]), prim[1][:8], prim[2][:8]

    state = inner(row(1))
    part = along(state, primitives(state), 0)
    full = row(2)
    full_prim = primitives(full)
    state, prim = inner(full), inner_prim(full_prim)
    next_part = along(state, prim, 0)
    faces = face(part, next_part)
    for i in range(2, 10):
        part = next_part
        next_full = row(i + 1)
        next_full_prim = primitives(next_full)
        next_state, next_prim = inner(next_full), inner_prim(next_full_prim)
        next_part = along(next_state, next_prim, 0)
        next_faces = face(part, next_part)
        _, net_y = cyclic_net(full, full_prim, 1, 1, 0)
        net_z = closed_net(along(state, prim, 2), inflow_two, i)
        total = [b - a + y[:8] + z for a, b, y, z in zip(faces, next_faces, net_y, net_z, strict=True)]
        for c, v in enumerate(advanced(state, prim, total)):
            stepped[c, i - 2] = 0.5 * box[c, i, 0:8] + 0.5 * v
        full, full_prim, state, prim, faces = next_full, next_full_prim, next_state, next_prim, next_faces


def two_parts(v):
    big = v.astype(BF16)
    return big, (v - big.astype(F32)).astype(BF16)


def split_cell(cells):
    return (cells >> 7) & 31, ((cells >> 12) << 7) | (cells & 127)


def one_hot(index, count):
    return jnp.where(sublane((count, index.shape[-1])) == index, 1.0, 0.0)


def gather_update(order, counts, box, own, below, above, parcels, cells, stepped, sources, updated, front, back, ahead, table, carried, live):
    gas_step(box, own, below, above, stepped, ahead)

    for c in range(6):
        left, right = (jnp.reshape(stepped[c, x : x + 4], (32, 128)) for x in (0, 4))
        big, small = two_parts(jnp.concatenate([left, right], axis=1))
        table[pl.ds(32 * c, 32), :] = big
        table[pl.ds(192 + 32 * c, 32), :] = small

    def chunk(n, _):
        index = cells[pl.ds(2 * n, 2), :]
        index = jnp.concatenate([index[0:1], index[1:2]], axis=1)
        row, column = split_cell(index)
        found = jnp.dot(table[...], one_hot(column, 256).astype(BF16), preferred_element_type=F32)
        chosen = sublane((32, 256)) == row
        for c in range(6):
            both = found[32 * c : 32 * c + 32] + found[192 + 32 * c : 224 + 32 * c]
            value = jnp.sum(jnp.where(chosen, both, 0.0), axis=0, keepdims=True)
            carried[c, pl.ds(2 * n, 1), :] = value[:, :128]
            carried[c, pl.ds(2 * n + 1, 1), :] = value[:, 128:]
        return 0

    lax.fori_loop(0, 32, chunk, 0)

    kept, forward, backward = counts[0, 0], counts[0, 1], counts[0, 2]

    def mark(j, _):
        alive = jnp.where(j < kept + forward + backward, 1.0, 0.0)
        live[pl.ds(order[0, j], 1), :] = jnp.full((1, 128), alive, F32)
        return 0

    lax.fori_loop(0, 64, mark, 0)

    r, m1, m2, m3, e, q = (carried[c] for c in range(6))
    inv = 1.0 / r
    g = (m1 * inv, m2 * inv, m3 * inv)
    t = (GAMMA - 1.0) * (e - 0.5 * (m1 * g[0] + m2 * g[1] + m3 * g[2])) * inv
    y = q * inv
    v = tuple(parcels[:, k, :] for k in range(3))
    mass, heat = parcels[:, 3, :], parcels[:, 4, :]
    root = jnp.sqrt(mass)
    inv_root = 1.0 / root
    new_mass = mass * jnp.exp(-TIME_STEP * EVAP_RATE * t / (root * (1.0 + y * y)))
    slow = jnp.exp((-TIME_STEP / DRAG_RELAX_TIME) * inv_root)
    new_v = tuple(gk + (vk - gk) * slow for gk, vk in zip(g, v, strict=True))
    new_heat = t + (heat - t) * jnp.exp((-TIME_STEP / HEATING_RELAX) * inv_root)
    alive = live[...]
    sources[0] = (mass - new_mass) * alive
    for k in range(3):
        sources[1 + k] = (mass * v[k] - new_mass * new_v[k]) * alive
    square = v[0] * v[0] + v[1] * v[1] + v[2] * v[2]
    new_square = new_v[0] * new_v[0] + new_v[1] * new_v[1] + new_v[2] * new_v[2]
    sources[4] = (
        0.5 * (mass * square - new_mass * new_square) + LIQUID_HEAT * (mass * heat - new_mass * new_heat)
    ) * alive
    for k in range(3):
        updated[:, k, :] = new_v[k]
    updated[:, 3, :] = new_mass
    updated[:, 4, :] = new_heat
    for k in range(5, 8):
        updated[:, k, :] = jnp.zeros((64, 128), F32)

    row_five = sublane((8, 128)) == 5
    for out, start, size in ((front, kept, forward), (back, kept + forward, backward)):

        def send(j, _, out=out, start=start, size=size):
            block = updated[order[0, jnp.minimum(start + j, 63)]]
            out[j] = jnp.where(row_five, size.astype(F32), block)
            return 0

        lax.fori_loop(0, 16, send, 0)


def scatter(stepped, sources, cells, gas_out):
    total = None
    for n in range(8):
        columns, big, small = [], [], []
        for b in range(8 * n, 8 * n + 8):
            row, column = split_cell(cells[b : b + 1, :])
            columns.append(one_hot(column, 256).astype(BF16))
            chosen = sublane((32, 128)) == row
            wide = [
                jnp.where(chosen, jnp.broadcast_to(sources[c, b : b + 1, :], (32, 128)), 0.0) for c in range(5)
            ]
            wide = two_parts(jnp.concatenate(wide, axis=0))
            big.append(wide[0])
            small.append(wide[1])
        left = jnp.concatenate([jnp.concatenate(big, axis=1), jnp.concatenate(small, axis=1)], axis=0)
        part = lax.dot_general(
            left, jnp.concatenate(columns, axis=1), (((1,), (1,)), ((), ())), preferred_element_type=F32
        )
        total = part if total is None else total + part
    for c in range(6):
        k = c % 5
        both = total[32 * k : 32 * k + 32] + total[160 + 32 * k : 192 + 32 * k]
        for half in range(2):
            added = jnp.reshape(both[:, 128 * half : 128 * half + 128], (4, 8, 128))
            gas_out[c, 4 * half : 4 * half + 4] = stepped[c, 4 * half : 4 * half + 4] + added


def place(order, counts, updated, lower, upper, moved):
    kept = counts[0, 0]
    has_lower = jnp.logical_not(ends("gx")[0])
    has_upper = jnp.logical_not(ends("gx")[1])
    from_lower = jnp.where(has_lower, lower[0, 5, 0], 0.0).astype(jnp.int32)
    from_upper = jnp.where(has_upper, upper[0, 5, 0], 0.0).astype(jnp.int32)
    moved[...] = jnp.zeros((64, 5, 128), F32)

    def own(j, _):
        moved[j] = updated[order[0, j]][:5]
        return 0

    def low(j, _):
        moved[kept + j] = lower[j][:5]
        return 0

    def high(j, _):
        moved[kept + from_lower + j] = upper[j][:5]
        return 0

    lax.fori_loop(0, kept, own, 0)
    lax.fori_loop(0, from_lower, low, 0)
    lax.fori_loop(0, from_upper, high, 0)


def body(gas, parcels, home_cell_index, order, counts):
    smem = pl.BlockSpec(memory_space=pltpu.SMEM)
    vmem = pl.BlockSpec(memory_space=pltpu.VMEM)
    xlo = shifted(gas[:, 6:8], "gx", 1)
    xhi = shifted(gas[:, 0:2], "gx", -1)
    rows, low, high = call(pack_y, [(6, 4, 8, 128), (6, 3, 8, 128), (6, 3, 8, 128)])(gas, xlo, xhi)
    ylo = shifted(high, "gy", 1)
    yhi = shifted(low, "gy", -1)
    box, pay = call(pack_z, [(6, 12, 16, 128), (6, 16, 128)])(gas, rows, ylo, yhi)
    below = shifted(pay, "gz", 1)
    above = shifted(pay, "gz", -1)
    stepped, sources, updated, front, back = call(
        gather_update,
        [(6, 8, 8, 128), (5, 64, 128), (64, 8, 128), (16, 8, 128), (16, 8, 128)],
        in_specs=[smem, smem] + [vmem] * 6,
        scratch_shapes=[
            pltpu.VMEM((6, 12, 16, 128), F32),
            pltpu.VMEM((384, 256), BF16),
            pltpu.VMEM((6, 64, 128), F32),
            pltpu.VMEM((64, 128), F32),
        ],
    )(order, counts, box, pay, below, above, parcels, home_cell_index)
    lower = shifted(front, "gx", 1)
    upper = shifted(back, "gx", -1)
    (gas_out,) = call(scatter, [(6, 8, 8, 128)])(stepped, sources, home_cell_index)
    (moved,) = call(place, [(64, 5, 128)], in_specs=[smem, smem] + [vmem] * 3)(order, counts, updated, lower, upper)
    return gas_out, moved


def solution(mesh):
    blocks = ("gx", "gy", "gz")
    in_specs = (
        P(None, *blocks),
        P(blocks, None, None),
        P(blocks, None),
        P(blocks, None),
        P(blocks, None),
    )
    out_specs = (P(None, *blocks), P(blocks, None, None))
    return jax.shard_map(body, mesh=mesh, in_specs=in_specs, out_specs=out_specs, check_vma=False)
```

```python
import jax
import jax.numpy as jnp
from jax import lax
from jax.experimental import pallas as pl
from jax.experimental.pallas import tpu as pltpu
from jax.sharding import PartitionSpec as P

GAMMA = 1.4
TIME_STEP = 0.1
RATE = 3.0
ACTIVATION = 2.0
HEAT = 5.0
DRAG_RELAX_TIME = 0.4
HEATING_RELAX = 0.6
EVAP_RATE = 1.5
LIQUID_HEAT = 2.0

F32 = jnp.float32
BF16 = jnp.bfloat16
INTERPRET = False


def shifted(block, axis, step):
    count = lax.axis_size(axis)
    return lax.ppermute(block, axis, [(i, i + step) for i in range(count) if 0 <= i + step < count])


def ends(axis):
    at = lax.axis_index(axis)
    return at == 0, at == lax.axis_size(axis) - 1


def call(kernel, outs, scalars, arrays, to=pltpu.VMEM, **kwargs):
    outs = [out if isinstance(out[0], tuple) else (out, F32) for out in outs]
    specs = [pl.BlockSpec(memory_space=pltpu.SMEM)] * len(scalars)
    specs += [pl.BlockSpec(memory_space=pltpu.VMEM)] * len(arrays)
    if not INTERPRET:
        arrays = [pltpu.with_memory_space_constraint(a, pltpu.VMEM) for a in arrays]
    make = jax.ShapeDtypeStruct if INTERPRET else to
    return pl.pallas_call(
        kernel,
        out_shape=[make(shape, dtype) for shape, dtype in outs],
        in_specs=specs,
        out_specs=[pl.BlockSpec(memory_space=pltpu.VMEM)] * len(outs),
        interpret=INTERPRET,
        **kwargs,
    )(*scalars, *arrays)


def sublane(shape):
    return lax.broadcasted_iota(jnp.int32, shape, len(shape) - 2)


def lane(shape):
    return lax.broadcasted_iota(jnp.int32, shape, len(shape) - 1)


def turn(v, shift, axis):
    size = v.shape[axis]
    shift %= size
    return v if shift == 0 else pltpu.roll(v, shift, axis)


def pack_y(gas, xlo, xhi, rows, low_pay, high_pay):
    first, last = ends("gx")
    sub = sublane((8, 128))
    for c in range(6):
        line = []
        for i in range(12):
            if i < 2:
                line.append(jnp.where(first, gas[c, 0], xlo[c, i]))
                rows[c, i] = line[-1]
            elif i < 10:
                line.append(gas[c, i - 2])
            else:
                line.append(jnp.where(last, gas[c, 7], xhi[c, i - 10]))
                rows[c, i - 8] = line[-1]
        for g in range(3):
            low = line[4 * g]
            high = turn(line[4 * g], 2, 0)
            for k in range(1, 4):
                here = (sub >= 2 * k) & (sub < 2 * k + 2)
                low = jnp.where(here, turn(line[4 * g + k], 2 * k, 0), low)
                high = jnp.where(here, turn(line[4 * g + k], 2 * k + 2, 0), high)
            low_pay[c, g] = low
            high_pay[c, g] = high


def pack_z(gas, rows, ylo, yhi, box, pay):
    first, last = ends("gy")
    sub = sublane((8, 128))
    group = lane((16, 128)) // 8
    for c in range(6):
        packed = None
        for i in range(12):
            if 2 <= i < 10:
                mid = gas[c, i - 2]
            else:
                mid = rows[c, i if i < 2 else i - 8]
            g, k = i // 4, i % 4
            below = turn(ylo[c, g], 6 - 2 * k, 0)
            above = turn(yhi[c, g], -2 * k, 0)
            below = jnp.where(first, jnp.broadcast_to(mid[0:1], (8, 128)), below)
            above = jnp.where(last, jnp.broadcast_to(mid[7:8], (8, 128)), above)
            line = jnp.concatenate([mid, jnp.where(sub < 4, above, below)], axis=0)
            box[c, i] = line
            moved = turn(line, 8 * i + 2, 1)
            packed = moved if packed is None else jnp.where(group == i, moved, packed)
        pay[c] = packed


def primitives(state):
    r, m1, m2, m3, e, _ = state
    inv = 1.0 / r
    u = (m1 * inv, m2 * inv, m3 * inv)
    p = (GAMMA - 1.0) * (e - 0.5 * (m1 * u[0] + m2 * u[1] + m3 * u[2]))
    return u, p, jnp.sqrt(GAMMA * p * inv)


def along(state, prim, k):
    u, p, sound = prim
    uk = u[k]
    flux = [state[1 + k], state[1] * uk, state[2] * uk, state[3] * uk, (state[4] + p) * uk, state[5] * uk]
    flux[1 + k] = flux[1 + k] + p
    return flux, jnp.abs(uk) + sound, state


def face(lower, upper):
    speed = jnp.maximum(lower[1], upper[1])
    return [
        (fa + fb) - speed * (b - a)
        for fa, fb, a, b in zip(lower[0], upper[0], lower[2], upper[2], strict=True)
    ]


def over(part, move):
    flux, speed, state = part
    return [move(f) for f in flux], move(speed), [move(v) for v in state]


def advanced(state, prim, total):
    burned = RATE * state[5] * jnp.exp(-ACTIVATION * state[0] / prim[1])
    out = [v - (0.5 * TIME_STEP) * t for v, t in zip(state, total, strict=True)]
    out[4] = out[4] + (TIME_STEP * HEAT) * burned
    out[5] = out[5] - TIME_STEP * burned
    return out


def cyclic_net(state, prim, k, distance, axis):
    part = along(state, prim, k)
    faces = face(part, over(part, lambda v: turn(v, -distance, axis)))
    return faces, [f - turn(f, distance, axis) for f in faces]


def side_state(own, below, above, first, last):
    at = lane((16, 128)) % 8
    low = jnp.where(at < 2, jnp.where(first, jnp.where(at == 0, turn(own, -2, 1), turn(own, -1, 1)), below), own)
    high = jnp.where(at < 2, own, jnp.where(last, jnp.where(at == 2, turn(own, 1, 1), turn(own, 2, 1)), above))
    return jnp.where(at < 4, low, turn(high, 4, 1))


def side_inflow(faces):
    at = lane((16, 128)) % 8
    return [jnp.where(at == 0, turn(f, -5, 1), -f) for f in faces]


def closed_net(part):
    faces = face(part, over(part, lambda v: turn(v, -1, 1)))
    faces = [jnp.where(lane(f.shape) == 127, 0.0, f) for f in faces]
    return [f - turn(f, 1, 1) for f in faces]


def outer(inflow, i):
    at = lane(inflow.shape)
    return jnp.where((at == 0) | (at == 127), turn(inflow, 127 - 8 * i, 1), 0.0)


def clamp_y(v):
    first, last = ends("gy")
    sub = sublane(v.shape)
    v = jnp.where(first & (sub == 15), jnp.broadcast_to(v[0:1], v.shape), v)
    return jnp.where(last & (sub == 8), jnp.broadcast_to(v[7:8], v.shape), v)


def stage_one(box, ahead):
    state = [box[c, 0] for c in range(6)]
    part = along(state, primitives(state), 0)
    state = [box[c, 1] for c in range(6)]
    prim = primitives(state)
    next_part = along(state, prim, 0)
    faces = face(part, next_part)
    for i in range(1, 11):
        part = next_part
        next_state = [box[c, i + 1] for c in range(6)]
        next_prim = primitives(next_state)
        next_part = along(next_state, next_prim, 0)
        next_faces = face(part, next_part)
        _, net_y = cyclic_net(state, prim, 1, 1, 0)
        net_z = closed_net(along(state, prim, 2))
        total = [b - a + y + z for a, b, y, z in zip(faces, next_faces, net_y, net_z, strict=True)]
        for c, v in enumerate(advanced(state, prim, total)):
            ahead[c, i] = v
        state, prim, faces = next_state, next_prim, next_faces


def sides(own, below, above):
    first_x, last_x = ends("gx")
    first_z, last_z = ends("gz")
    at = lane((16, 128)) % 8
    group = lane((16, 128)) // 8

    def clamp_x_z(v):
        v = jnp.where(first_x & (group == 1), turn(v, -8, 1), v)
        v = jnp.where(last_x & (group == 10), turn(v, 8, 1), v)
        v = jnp.where(first_z & (at == 1), turn(v, -1, 1), v)
        return jnp.where(last_z & (at == 6), turn(v, 1, 1), v)

    side = [side_state(own[c], below[c], above[c], first_z, last_z) for c in range(6)]
    prim = primitives(side)
    faces, net_z = cyclic_net(side, prim, 2, 1, 1)
    one = side_inflow(faces)
    _, net_x = cyclic_net(side, prim, 0, 8, 1)
    _, net_y = cyclic_net(side, prim, 1, 1, 0)
    side = advanced(side, prim, [x + y + z for x, y, z in zip(net_x, net_y, net_z, strict=True)])
    side = [clamp_y(clamp_x_z(v)) for v in side]
    return one, side_inflow(cyclic_net(side, primitives(side), 2, 1, 1)[0])


def stage_two(box, ahead, one, two, stepped, fields):
    first_x, last_x = ends("gx")

    def line(i):
        out = []
        for c in range(6):
            out.append(clamp_y(ahead[c, i] - (0.5 * TIME_STEP) * outer(one[c], i)))
        return out

    def row(i):
        v = line(i)
        if i == 1:
            v = [jnp.where(first_x, b, a) for a, b in zip(v, line(2), strict=True)]
        if i == 10:
            v = [jnp.where(last_x, b, a) for a, b in zip(v, line(9), strict=True)]
        return v

    def inner(values):
        return [v[:8] for v in values]

    def inner_prim(prim):
        return inner(prim[0]), prim[1][:8], prim[2][:8]

    state = inner(row(1))
    part = along(state, primitives(state), 0)
    full = row(2)
    full_prim = primitives(full)
    state, prim = inner(full), inner_prim(full_prim)
    next_part = along(state, prim, 0)
    faces = face(part, next_part)
    for i in range(2, 10):
        part = next_part
        next_full = row(i + 1)
        next_full_prim = primitives(next_full)
        next_state, next_prim = inner(next_full), inner_prim(next_full_prim)
        next_part = along(next_state, next_prim, 0)
        next_faces = face(part, next_part)
        _, net_y = cyclic_net(full, full_prim, 1, 1, 0)
        net_z = closed_net(along(state, prim, 2))
        total = [
            b - a + y[:8] + z + outer(s[:8], i)
            for a, b, y, z, s in zip(faces, next_faces, net_y, net_z, two, strict=True)
        ]
        x = i - 2
        done = [0.5 * box[c, i, 0:8] + 0.5 * v for c, v in enumerate(advanced(state, prim, total))]
        for c in range(6):
            stepped[c, x] = done[c]
        inv = 1.0 / done[0]
        g = [done[1 + k] * inv for k in range(3)]
        t = (GAMMA - 1.0) * (done[4] - 0.5 * (done[1] * g[0] + done[2] * g[1] + done[3] * g[2])) * inv
        for f, v in enumerate((*g, t, done[5] * inv)):
            fields[f, pl.ds(8 * (x % 4), 8), pl.ds(128 * (x // 4), 128)] = v
        full, full_prim, state, prim, faces = next_full, next_full_prim, next_state, next_prim, next_faces


def two_parts(v):
    big = v.astype(BF16)
    return big, (v - big.astype(F32)).astype(BF16)


def split_cell(cells):
    return (cells >> 7) & 31, ((cells >> 12) << 7) | (cells & 127)


def one_hot(index, count):
    return jnp.where(sublane((count, index.shape[-1])) == index, 1.0, 0.0).astype(BF16)


def in_order(order, parcels, cells, sorted_parcels, sorted_cells):
    for j in range(64):
        b = order[0, j]
        sorted_cells[j : j + 1, :] = cells[pl.ds(b, 1), :]
        for k in range(5):
            sorted_parcels[k, j : j + 1, :] = parcels[k, pl.ds(b, 1), :]


def alive(counts):
    return counts[0, 0] + counts[0, 1] + counts[0, 2]


def gather_update(counts, box, ahead, own, below, above, parcels, cells, stepped, sources, updated, front, back, fields, table, carried):
    one, two = sides(own, below, above)
    stage_two(box, ahead, one, two, stepped, fields)
    for f in range(5):
        big, small = two_parts(fields[f])
        table[pl.ds(32 * f, 32), :] = big
        table[pl.ds(160 + 32 * f, 32), :] = small

    total = alive(counts)

    def chunk(n, _):
        start = pl.multiple_of(8 * n, 8)
        index = cells[pl.ds(start, 8), :]
        values = [[] for _ in range(5)]
        for b in range(0, 8, 2):
            pair = jnp.concatenate([index[b : b + 1], index[b + 1 : b + 2]], axis=1)
            row, column = split_cell(pair)
            found = jnp.dot(table[...], one_hot(column, 256), preferred_element_type=F32)
            chosen = sublane((32, 256)) == row
            for f in range(5):
                both = found[32 * f : 32 * f + 32] + found[160 + 32 * f : 192 + 32 * f]
                value = jnp.sum(jnp.where(chosen, both, 0.0), axis=0, keepdims=True)
                values[f] += [value[:, :128], value[:, 128:]]
        for f in range(5):
            carried[f, pl.ds(start, 8), :] = jnp.concatenate(values[f], axis=0)
        return 0

    lax.fori_loop(0, (total + 7) // 8, chunk, 0)

    g = tuple(carried[k] for k in range(3))
    t, y = carried[3], carried[4]
    v = tuple(parcels[k] for k in range(3))
    mass, heat = parcels[3], parcels[4]
    root = jnp.sqrt(mass)
    inv_root = 1.0 / root
    new_mass = mass * jnp.exp((-TIME_STEP * EVAP_RATE) * t / (root * (1.0 + y * y)))
    slow = jnp.exp((-TIME_STEP / DRAG_RELAX_TIME) * inv_root)
    new_v = tuple(gk + (vk - gk) * slow for gk, vk in zip(g, v, strict=True))
    new_heat = t + (heat - t) * jnp.exp((-TIME_STEP / HEATING_RELAX) * inv_root)
    live = sublane((64, 128)) < total
    square = v[0] * v[0] + v[1] * v[1] + v[2] * v[2]
    new_square = new_v[0] * new_v[0] + new_v[1] * new_v[1] + new_v[2] * new_v[2]
    gain = [mass - new_mass]
    gain += [mass * v[k] - new_mass * new_v[k] for k in range(3)]
    gain += [0.5 * (mass * square - new_mass * new_square) + LIQUID_HEAT * (mass * heat - new_mass * new_heat)]
    for k in range(5):
        sources[k] = jnp.where(live, gain[k], 0.0)
    for k, value in enumerate((*new_v, new_mass, new_heat)):
        updated[k] = value

    kept, forward, backward = counts[0, 0], counts[0, 1], counts[0, 2]
    for out, start, size in ((front, kept, forward), (back, kept + forward, backward)):
        for k in range(5):
            out[k] = updated[k, pl.ds(start, 16), :]
        out[5] = jnp.full((16, 128), size.astype(F32))


def scatter(counts, stepped, sources, cells, gas_out, total):
    total[...] = jnp.zeros(total.shape, F32)

    def chunk(n, _):
        start = pl.multiple_of(8 * n, 8)
        index = cells[pl.ds(start, 8), :]
        given = [two_parts(sources[k, pl.ds(start, 8), :]) for k in range(5)]
        given = [[part.astype(F32) for part in parts] for parts in given]
        columns, wide = [], []
        for b in range(8):
            row, column = split_cell(index[b : b + 1, :])
            columns.append(one_hot(column, 256))
            chosen = sublane((32, 128)) == row
            wide.append(
                jnp.concatenate(
                    [
                        jnp.where(chosen, jnp.broadcast_to(given[k][half][b : b + 1, :], (32, 128)), 0.0).astype(BF16)
                        for half in range(2)
                        for k in range(5)
                    ],
                    axis=0,
                )
            )
        total[...] += lax.dot_general(
            jnp.concatenate(wide, axis=1),
            jnp.concatenate(columns, axis=1),
            (((1,), (1,)), ((), ())),
            preferred_element_type=F32,
        )
        return 0

    lax.fori_loop(0, (alive(counts) + 7) // 8, chunk, 0)
    for c in range(6):
        k = c % 5
        both = total[32 * k : 32 * k + 32] + total[160 + 32 * k : 192 + 32 * k]
        for half in range(2):
            added = jnp.reshape(both[:, 128 * half : 128 * half + 128], (4, 8, 128))
            gas_out[c, 4 * half : 4 * half + 4] = stepped[c, 4 * half : 4 * half + 4] + added


def place(counts, updated, lower, upper, moved):
    kept = counts[0, 0]
    first, last = ends("gx")
    from_lower = jnp.where(first, 0.0, lower[5, 0, 0]).astype(jnp.int32)
    from_upper = jnp.where(last, 0.0, upper[5, 0, 0]).astype(jnp.int32)
    slot = sublane((64, 128))
    near = sublane((16, 128))
    for k in range(5):
        moved[k] = jnp.where(slot < kept, updated[k], 0.0)
    for k in range(5):
        moved[k, pl.ds(kept, 16), :] = jnp.where(near < from_lower, lower[k], 0.0)
    for k in range(5):
        moved[k, pl.ds(kept + from_lower, 16), :] = jnp.where(near < from_upper, upper[k], 0.0)


def body(gas, parcels, home_cell_index, order, counts):
    xlo = shifted(gas[:, 6:8], "gx", 1)
    xhi = shifted(gas[:, 0:2], "gx", -1)
    sorted_parcels, cells = call(
        in_order, [(5, 64, 128), ((64, 128), jnp.int32)], [order], [jnp.transpose(parcels, (1, 0, 2)), home_cell_index]
    )
    rows, low, high = call(pack_y, [(6, 4, 8, 128), (6, 3, 8, 128), (6, 3, 8, 128)], [], [gas, xlo, xhi])
    ylo = shifted(high, "gy", 1)
    yhi = shifted(low, "gy", -1)
    box, pay = call(pack_z, [(6, 12, 16, 128), (6, 16, 128)], [], [gas, rows, ylo, yhi])
    below = shifted(pay, "gz", 1)
    above = shifted(pay, "gz", -1)
    (ahead,) = call(stage_one, [(6, 12, 16, 128)], [], [box])
    stepped, sources, updated, front, back = call(
        gather_update,
        [(6, 8, 8, 128), (5, 64, 128), (5, 64, 128), (6, 16, 128), (6, 16, 128)],
        [counts],
        [box, ahead, pay, below, above, sorted_parcels, cells],
        scratch_shapes=[
            pltpu.VMEM((5, 32, 256), F32),
            pltpu.VMEM((320, 256), BF16),
            pltpu.VMEM((5, 64, 128), F32),
        ],
    )
    lower = shifted(front, "gx", 1)
    upper = shifted(back, "gx", -1)
    (gas_out,) = call(
        scatter,
        [(6, 8, 8, 128)],
        [counts],
        [stepped, sources, cells],
        to=pltpu.HBM,
        scratch_shapes=[pltpu.VMEM((320, 256), F32)],
    )
    (moved,) = call(place, [(5, 64, 128)], [counts], [updated, lower, upper], to=pltpu.HBM)
    return gas_out, jnp.transpose(moved, (1, 0, 2))


def solution(mesh):
    blocks = ("gx", "gy", "gz")
    in_specs = (
        P(None, *blocks),
        P(blocks, None, None),
        P(blocks, None),
        P(blocks, None),
        P(blocks, None),
    )
    out_specs = (P(None, *blocks), P(blocks, None, None))
    return jax.shard_map(body, mesh=mesh, in_specs=in_specs, out_specs=out_specs, check_vma=False)
```

```python
import jax
import jax.numpy as jnp
from jax import lax
from jax.experimental import pallas as pl
from jax.experimental.pallas import tpu as pltpu
from jax.sharding import PartitionSpec as P


GAMMA = 1.4
TIME_STEP = 0.1
RATE = 3.0
ACTIVATION = 2.0
HEAT = 5.0
DRAG_RELAX_TIME = 0.4
HEATING_RELAX = 0.6
EVAP_RATE = 1.5
LIQUID_HEAT = 2.0

F32 = jnp.float32
BF16 = jnp.bfloat16
INTERPRET = False


def swapped(blocks, axis):
    count = lax.axis_size(axis)
    out = []
    for first, block in enumerate(blocks):
        pairs = [(i, i + 1) for i in range(first, count - 1, 2)]
        out.append(lax.ppermute(block, axis, pairs + [(j, i) for i, j in pairs]))
    return out


def is_even(axis):
    return lax.axis_index(axis) % 2 == 0


def ends(axis):
    at = lax.axis_index(axis)
    return at == 0, at == lax.axis_size(axis) - 1


def call(kernel, outs, scalars, arrays, to=None, **kwargs):
    outs = [out if isinstance(out[0], tuple) else (out, F32) for out in outs]
    specs = [pl.BlockSpec(memory_space=pltpu.SMEM)] * len(scalars)
    specs += [pl.BlockSpec(memory_space=pltpu.VMEM)] * len(arrays)
    if not INTERPRET:
        arrays = [pltpu.with_memory_space_constraint(a, pltpu.VMEM) for a in arrays]
    to = [jax.ShapeDtypeStruct if INTERPRET else space for space in to or [pltpu.VMEM] * len(outs)]
    return pl.pallas_call(
        kernel,
        out_shape=[space(*out) for space, out in zip(to, outs, strict=True)],
        in_specs=specs,
        out_specs=[pl.BlockSpec(memory_space=pltpu.VMEM)] * len(outs),
        interpret=INTERPRET,
        **kwargs,
    )(*scalars, *arrays)


def sublane(shape):
    return lax.broadcasted_iota(jnp.int32, shape, len(shape) - 2)


def lane(shape):
    return lax.broadcasted_iota(jnp.int32, shape, len(shape) - 1)


def turn(v, shift, axis):
    size = v.shape[axis]
    shift %= size
    return v if shift == 0 else pltpu.roll(v, shift, axis)


def pack_y(gas, even_pairs, odd_pairs, _, rows, even_pay, odd_pay):
    first, last = ends("gx")
    even_x, even_y = is_even("gx"), is_even("gy")
    sub = sublane((8, 128))
    for c in range(6):
        line = []
        for i in range(12):
            if i < 2:
                below = jnp.where(even_x, odd_pairs[c, i], even_pairs[c, i])
                line.append(jnp.where(first, gas[c, 0], below))
                rows[c, i] = line[-1]
            elif i < 10:
                line.append(gas[c, i - 2])
            else:
                above = jnp.where(even_x, even_pairs[c, i - 10], odd_pairs[c, i - 10])
                line.append(jnp.where(last, gas[c, 7], above))
                rows[c, i - 8] = line[-1]
        for g in range(3):
            low = line[4 * g]
            high = turn(line[4 * g], 2, 0)
            for k in range(1, 4):
                here = (sub >= 2 * k) & (sub < 2 * k + 2)
                low = jnp.where(here, turn(line[4 * g + k], 2 * k, 0), low)
                high = jnp.where(here, turn(line[4 * g + k], 2 * k + 2, 0), high)
            even_pay[c, g] = jnp.where(even_y, high, low)
            odd_pay[c, g] = jnp.where(even_y, low, high)


def pack_z(gas, rows, even_pairs, odd_pairs, box, pay):
    even = is_even("gy")
    first, last = ends("gy")
    sub = sublane((8, 128))
    group = lane((16, 128)) // 8
    for c in range(6):
        ylo = [jnp.where(even, odd_pairs[c, g], even_pairs[c, g]) for g in range(3)]
        yhi = [jnp.where(even, even_pairs[c, g], odd_pairs[c, g]) for g in range(3)]
        packed = None
        for i in range(12):
            if 2 <= i < 10:
                mid = gas[c, i - 2]
            else:
                mid = rows[c, i if i < 2 else i - 8]
            g, k = i // 4, i % 4
            below = turn(ylo[g], 6 - 2 * k, 0)
            above = turn(yhi[g], -2 * k, 0)
            below = jnp.where(first, jnp.broadcast_to(mid[0:1], (8, 128)), below)
            above = jnp.where(last, jnp.broadcast_to(mid[7:8], (8, 128)), above)
            line = jnp.concatenate([mid, jnp.where(sub < 4, above, below)], axis=0)
            box[c, i] = line
            moved = turn(line, 8 * i + 2, 1)
            packed = moved if packed is None else jnp.where(group == i, moved, packed)
        pay[c] = packed


def primitives(state):
    r, m1, m2, m3, e, _ = state
    inv = 1.0 / r
    u = (m1 * inv, m2 * inv, m3 * inv)
    p = (GAMMA - 1.0) * (e - 0.5 * (m1 * u[0] + m2 * u[1] + m3 * u[2]))
    return u, p, jnp.sqrt(GAMMA * p * inv)


def along(state, prim, k):
    u, p, sound = prim
    uk = u[k]
    flux = [state[1 + k], state[1] * uk, state[2] * uk, state[3] * uk, (state[4] + p) * uk, state[5] * uk]
    flux[1 + k] = flux[1 + k] + p
    return flux, jnp.abs(uk) + sound, state


def face(lower, upper):
    speed = jnp.maximum(lower[1], upper[1])
    return [
        (fa + fb) - speed * (b - a)
        for fa, fb, a, b in zip(lower[0], upper[0], lower[2], upper[2], strict=True)
    ]


def over(part, move):
    flux, speed, state = part
    return [move(f) for f in flux], move(speed), [move(v) for v in state]


def advanced(state, prim, total):
    burned = RATE * state[5] * jnp.exp(-ACTIVATION * state[0] / prim[1])
    out = [v - (0.5 * TIME_STEP) * t for v, t in zip(state, total, strict=True)]
    out[4] = out[4] + (TIME_STEP * HEAT) * burned
    out[5] = out[5] - TIME_STEP * burned
    return out


def cyclic_net(state, prim, k, distance, axis):
    part = along(state, prim, k)
    faces = face(part, over(part, lambda v: turn(v, -distance, axis)))
    return faces, [f - turn(f, distance, axis) for f in faces]


def side_state(own, below, above, first, last):
    at = lane((16, 128)) % 8
    low = jnp.where(at < 2, jnp.where(first, jnp.where(at == 0, turn(own, -2, 1), turn(own, -1, 1)), below), own)
    high = jnp.where(at < 2, own, jnp.where(last, jnp.where(at == 2, turn(own, 1, 1), turn(own, 2, 1)), above))
    return jnp.where(at < 4, low, turn(high, 4, 1))


def side_inflow(faces):
    at = lane((16, 128)) % 8
    return [jnp.where(at == 0, turn(f, -5, 1), -f) for f in faces]


def closed_net(part):
    faces = face(part, over(part, lambda v: turn(v, -1, 1)))
    faces = [jnp.where(lane(f.shape) == 127, 0.0, f) for f in faces]
    return [f - turn(f, 1, 1) for f in faces]


def outer(inflow, i):
    at = lane(inflow.shape)
    return jnp.where((at == 0) | (at == 127), turn(inflow, 127 - 8 * i, 1), 0.0)


def clamp_y(v):
    first, last = ends("gy")
    sub = sublane(v.shape)
    v = jnp.where(first & (sub == 15), jnp.broadcast_to(v[0:1], v.shape), v)
    return jnp.where(last & (sub == 8), jnp.broadcast_to(v[7:8], v.shape), v)


def stage_one(box, ahead):
    state = [box[c, 0] for c in range(6)]
    part = along(state, primitives(state), 0)
    state = [box[c, 1] for c in range(6)]
    prim = primitives(state)
    next_part = along(state, prim, 0)
    faces = face(part, next_part)
    for i in range(1, 11):
        part = next_part
        next_state = [box[c, i + 1] for c in range(6)]
        next_prim = primitives(next_state)
        next_part = along(next_state, next_prim, 0)
        next_faces = face(part, next_part)
        _, net_y = cyclic_net(state, prim, 1, 1, 0)
        net_z = closed_net(along(state, prim, 2))
        total = [b - a + y + z for a, b, y, z in zip(faces, next_faces, net_y, net_z, strict=True)]
        for c, v in enumerate(advanced(state, prim, total)):
            ahead[c, i] = v
        state, prim, faces = next_state, next_prim, next_faces


def sides(own, even_pairs, odd_pairs):
    first_x, last_x = ends("gx")
    first_z, last_z = ends("gz")
    at = lane((16, 128)) % 8
    group = lane((16, 128)) // 8

    def clamp_x_z(v):
        v = jnp.where(first_x & (group == 1), turn(v, -8, 1), v)
        v = jnp.where(last_x & (group == 10), turn(v, 8, 1), v)
        v = jnp.where(first_z & (at == 1), turn(v, -1, 1), v)
        return jnp.where(last_z & (at == 6), turn(v, 1, 1), v)

    even = is_even("gz")
    side = []
    for c in range(6):
        below = jnp.where(even, odd_pairs[c], even_pairs[c])
        above = jnp.where(even, even_pairs[c], odd_pairs[c])
        side.append(side_state(own[c], below, above, first_z, last_z))
    prim = primitives(side)
    faces, net_z = cyclic_net(side, prim, 2, 1, 1)
    one = side_inflow(faces)
    _, net_x = cyclic_net(side, prim, 0, 8, 1)
    _, net_y = cyclic_net(side, prim, 1, 1, 0)
    side = advanced(side, prim, [x + y + z for x, y, z in zip(net_x, net_y, net_z, strict=True)])
    side = [clamp_y(clamp_x_z(v)) for v in side]
    return one, side_inflow(cyclic_net(side, primitives(side), 2, 1, 1)[0])


def stage_two(box, ahead, one, two, stepped, fields):
    first_x, last_x = ends("gx")

    def line(i):
        out = []
        for c in range(6):
            out.append(clamp_y(ahead[c, i] - (0.5 * TIME_STEP) * outer(one[c], i)))
        return out

    def row(i):
        v = line(i)
        if i == 1:
            v = [jnp.where(first_x, b, a) for a, b in zip(v, line(2), strict=True)]
        if i == 10:
            v = [jnp.where(last_x, b, a) for a, b in zip(v, line(9), strict=True)]
        return v

    def inner(values):
        return [v[:8] for v in values]

    def inner_prim(prim):
        return inner(prim[0]), prim[1][:8], prim[2][:8]

    state = inner(row(1))
    part = along(state, primitives(state), 0)
    full = row(2)
    full_prim = primitives(full)
    state, prim = inner(full), inner_prim(full_prim)
    next_part = along(state, prim, 0)
    faces = face(part, next_part)
    for i in range(2, 10):
        part = next_part
        next_full = row(i + 1)
        next_full_prim = primitives(next_full)
        next_state, next_prim = inner(next_full), inner_prim(next_full_prim)
        next_part = along(next_state, next_prim, 0)
        next_faces = face(part, next_part)
        _, net_y = cyclic_net(full, full_prim, 1, 1, 0)
        net_z = closed_net(along(state, prim, 2))
        total = [
            b - a + y[:8] + z + outer(s[:8], i)
            for a, b, y, z, s in zip(faces, next_faces, net_y, net_z, two, strict=True)
        ]
        x = i - 2
        done = [0.5 * box[c, i, 0:8] + 0.5 * v for c, v in enumerate(advanced(state, prim, total))]
        for c in range(6):
            stepped[c, x] = done[c]
        inv = 1.0 / done[0]
        g = [done[1 + k] * inv for k in range(3)]
        t = (GAMMA - 1.0) * (done[4] - 0.5 * (done[1] * g[0] + done[2] * g[1] + done[3] * g[2])) * inv
        for f, v in enumerate((*g, t, done[5] * inv)):
            fields[f, pl.ds(8 * (x % 4), 8), pl.ds(128 * (x // 4), 128)] = v
        full, full_prim, state, prim, faces = next_full, next_full_prim, next_state, next_prim, next_faces


def two_parts(v):
    big = v.astype(BF16)
    return big, (v - big.astype(F32)).astype(BF16)


def split_cell(cells):
    return (cells >> 7) & 31, ((cells >> 12) << 7) | (cells & 127)


def one_hot(index, count):
    return jnp.where(sublane((count, index.shape[-1])) == index, 1.0, 0.0).astype(BF16)


def moving(counts):
    return counts[0, 1] + counts[0, 2]


def alive(counts):
    return counts[0, 0] + moving(counts)


def in_order(order, counts, parcels, cells, sorted_parcels, sorted_cells):
    kept, moves, total = counts[0, 0], moving(counts), alive(counts)
    for j in range(64):
        b = order[0, jnp.where(j < moves, kept + j, jnp.where(j < total, j - moves, j))]
        sorted_cells[j : j + 1, :] = cells[pl.ds(b, 1), :]
        for k in range(5):
            sorted_parcels[k, j : j + 1, :] = parcels[k, pl.ds(b, 1), :]


def gather(table, cells, carried, begin, end):
    def chunk(n, _):
        start = pl.multiple_of(8 * n, 8)
        index = cells[pl.ds(start, 8), :]
        values = [[] for _ in range(5)]
        for b in range(0, 8, 2):
            pair = jnp.concatenate([index[b : b + 1], index[b + 1 : b + 2]], axis=1)
            row, column = split_cell(pair)
            found = jnp.dot(table[...], one_hot(column, 256), preferred_element_type=F32)
            chosen = sublane((32, 256)) == row
            for f in range(5):
                both = found[32 * f : 32 * f + 32] + found[160 + 32 * f : 192 + 32 * f]
                value = jnp.sum(jnp.where(chosen, both, 0.0), axis=0, keepdims=True)
                values[f] += [value[:, :128], value[:, 128:]]
        for f in range(5):
            carried[f, pl.ds(start, 8), :] = jnp.concatenate(values[f], axis=0)
        return 0

    lax.fori_loop(begin, end, chunk, 0)


def parcel_update(carried, parcels, rows):
    g = tuple(carried[k, :rows] for k in range(3))
    t, y = carried[3, :rows], carried[4, :rows]
    v = tuple(parcels[k, :rows] for k in range(3))
    mass, heat = parcels[3, :rows], parcels[4, :rows]
    root = jnp.sqrt(mass)
    inv_root = 1.0 / root
    new_mass = mass * jnp.exp((-TIME_STEP * EVAP_RATE) * t / (root * (1.0 + y * y)))
    slow = jnp.exp((-TIME_STEP / DRAG_RELAX_TIME) * inv_root)
    new_v = tuple(gk + (vk - gk) * slow for gk, vk in zip(g, v, strict=True))
    new_heat = t + (heat - t) * jnp.exp((-TIME_STEP / HEATING_RELAX) * inv_root)
    return (*v, mass, heat), (*new_v, new_mass, new_heat)


def parcel_sources(old, new):
    mass, new_mass = old[3], new[3]
    square = old[0] * old[0] + old[1] * old[1] + old[2] * old[2]
    new_square = new[0] * new[0] + new[1] * new[1] + new[2] * new[2]
    gain = [mass - new_mass]
    gain += [mass * old[k] - new_mass * new[k] for k in range(3)]
    gain += [0.5 * (mass * square - new_mass * new_square) + LIQUID_HEAT * (mass * old[4] - new_mass * new[4])]
    return gain


def gas_and_moving(
    counts, box, ahead, own, even_pairs, odd_pairs, parcels, cells,
    stepped, table, carried, even_pay, odd_pay, fields, updated,
):
    one, two = sides(own, even_pairs, odd_pairs)
    stage_two(box, ahead, one, two, stepped, fields)
    for f in range(5):
        big, small = two_parts(fields[f])
        table[pl.ds(32 * f, 32), :] = big
        table[pl.ds(160 + 32 * f, 32), :] = small
    gather(table, cells, carried, 0, (moving(counts) + 7) // 8)
    for k, value in enumerate(parcel_update(carried, parcels, 32)[1]):
        updated[k, 0:32] = value
        updated[k, 32:48] = jnp.zeros((16, 128), F32)

    even = is_even("gx")
    forward, backward = counts[0, 1], counts[0, 2]
    for out, up in ((even_pay, even), (odd_pay, jnp.logical_not(even))):
        start = jnp.where(up, 0, forward)
        for k in range(5):
            out[k] = updated[k, pl.ds(start, 16), :]
        out[5] = jnp.full((16, 128), jnp.where(up, forward, backward).astype(F32))


def kept_and_sources(counts, stepped, table, early, parcels, cells, gas_out, updated, carried, sources, total):
    carried[:, 0:32] = early[...]
    chunks = (alive(counts) + 7) // 8
    gather(table, cells, carried, (moving(counts) + 7) // 8, chunks)
    old, new = parcel_update(carried, parcels, 64)
    live = sublane((64, 128)) < alive(counts)
    for k, value in enumerate(parcel_sources(old, new)):
        sources[k] = jnp.where(live, value, 0.0)
        updated[k] = new[k]
    total[...] = jnp.zeros(total.shape, F32)

    def chunk(n, _):
        start = pl.multiple_of(8 * n, 8)
        index = cells[pl.ds(start, 8), :]
        given = [two_parts(sources[k, pl.ds(start, 8), :]) for k in range(5)]
        given = [[part.astype(F32) for part in parts] for parts in given]
        columns, wide = [], []
        for b in range(8):
            row, column = split_cell(index[b : b + 1, :])
            columns.append(one_hot(column, 256))
            chosen = sublane((32, 128)) == row
            wide.append(
                jnp.concatenate(
                    [
                        jnp.where(chosen, jnp.broadcast_to(given[k][half][b : b + 1, :], (32, 128)), 0.0).astype(BF16)
                        for half in range(2)
                        for k in range(5)
                    ],
                    axis=0,
                )
            )
        total[...] += lax.dot_general(
            jnp.concatenate(wide, axis=1),
            jnp.concatenate(columns, axis=1),
            (((1,), (1,)), ((), ())),
            preferred_element_type=F32,
        )
        return 0

    lax.fori_loop(0, chunks, chunk, 0)
    for c in range(6):
        k = c % 5
        both = total[32 * k : 32 * k + 32] + total[160 + 32 * k : 192 + 32 * k]
        for half in range(2):
            added = jnp.reshape(both[:, 128 * half : 128 * half + 128], (4, 8, 128))
            gas_out[c, 4 * half : 4 * half + 4] = stepped[c, 4 * half : 4 * half + 4] + added


def place(counts, updated, even_pairs, odd_pairs, moved):
    kept, moves = counts[0, 0], moving(counts)
    first, last = ends("gx")
    even = is_even("gx")
    from_lower = jnp.where(first, 0.0, jnp.where(even, odd_pairs[5, 0, 0], even_pairs[5, 0, 0])).astype(jnp.int32)
    from_upper = jnp.where(last, 0.0, jnp.where(even, even_pairs[5, 0, 0], odd_pairs[5, 0, 0])).astype(jnp.int32)
    slot = sublane((32, 128))
    near = sublane((16, 128))
    for k in range(5):
        moved[k, 0:32] = jnp.where(slot < kept, updated[k, pl.ds(moves, 32), :], 0.0)
        moved[k, 32:64] = jnp.zeros((32, 128), F32)
    for k in range(5):
        lower = jnp.where(even, odd_pairs[k], even_pairs[k])
        moved[k, pl.ds(kept, 16), :] = jnp.where(near < from_lower, lower, 0.0)
    for k in range(5):
        upper = jnp.where(even, even_pairs[k], odd_pairs[k])
        moved[k, pl.ds(kept + from_lower, 16), :] = jnp.where(near < from_upper, upper, 0.0)


def body(gas, parcels, home_cell_index, order, counts):
    even = is_even("gx")
    edges = [
        lax.dynamic_slice_in_dim(gas, jnp.where(even, near, far), 2, 1) for near, far in ((6, 0), (0, 6))
    ]
    x_halo = swapped(edges, "gx")
    sorted_parcels, cells = call(
        in_order,
        [(5, 64, 128), ((64, 128), jnp.int32)],
        [order, counts],
        [jnp.transpose(parcels, (1, 0, 2)), home_cell_index],
    )
    rows, *pays = call(pack_y, [(6, 4, 8, 128), (6, 3, 8, 128), (6, 3, 8, 128)], [], [gas, *x_halo, cells])
    y_halo = swapped(pays, "gy")
    box, pay = call(pack_z, [(6, 12, 16, 128), (6, 16, 128)], [], [gas, rows, *y_halo])
    z_halo = swapped([pay, pay], "gz")
    (ahead,) = call(stage_one, [(6, 12, 16, 128)], [], [box])
    stepped, table, carried, *pays = call(
        gas_and_moving,
        [(6, 8, 8, 128), ((320, 256), BF16), (5, 32, 128), (6, 16, 128), (6, 16, 128)],
        [counts],
        [box, ahead, pay, *z_halo, sorted_parcels, cells],
        scratch_shapes=[pltpu.VMEM((5, 32, 256), F32), pltpu.VMEM((5, 48, 128), F32)],
    )
    arrived = swapped(pays, "gx")
    gas_out, updated = call(
        kept_and_sources,
        [(6, 8, 8, 128), (5, 64, 128)],
        [counts],
        [stepped, table, carried, sorted_parcels, cells],
        to=[pltpu.HBM, pltpu.VMEM],
        scratch_shapes=[
            pltpu.VMEM((5, 64, 128), F32),
            pltpu.VMEM((5, 64, 128), F32),
            pltpu.VMEM((320, 256), F32),
        ],
    )
    (moved,) = call(place, [(5, 64, 128)], [counts], [updated, *arrived], to=[pltpu.HBM])
    return gas_out, jnp.transpose(moved, (1, 0, 2))


def solution(mesh):
    blocks = ("gx", "gy", "gz")
    in_specs = (
        P(None, *blocks),
        P(blocks, None, None),
        P(blocks, None),
        P(blocks, None),
        P(blocks, None),
    )
    out_specs = (P(None, *blocks), P(blocks, None, None))
    return jax.shard_map(body, mesh=mesh, in_specs=in_specs, out_specs=out_specs, check_vma=False)
```

```python
import jax
import jax.numpy as jnp
from jax import lax
from jax.experimental import pallas as pl
from jax.experimental.pallas import tpu as pltpu
from jax.sharding import PartitionSpec as P


GAMMA = 1.4
TIME_STEP = 0.1
RATE = 3.0
ACTIVATION = 2.0
HEAT = 5.0
DRAG_RELAX_TIME = 0.4
HEATING_RELAX = 0.6
EVAP_RATE = 1.5
LIQUID_HEAT = 2.0

F32 = jnp.float32
BF16 = jnp.bfloat16
INTERPRET = False


def swapped(blocks, axis):
    count = lax.axis_size(axis)
    out = []
    for first, block in enumerate(blocks):
        pairs = [(i, i + 1) for i in range(first, count - 1, 2)]
        out.append(lax.ppermute(block, axis, pairs + [(j, i) for i, j in pairs]))
    return out


def is_even(axis):
    return lax.axis_index(axis) % 2 == 0


def ends(axis):
    at = lax.axis_index(axis)
    return at == 0, at == lax.axis_size(axis) - 1


def call(kernel, outs, scalars, arrays, to=None, **kwargs):
    outs = [out if isinstance(out[0], tuple) else (out, F32) for out in outs]
    specs = [pl.BlockSpec(memory_space=pltpu.SMEM)] * len(scalars)
    specs += [pl.BlockSpec(memory_space=pltpu.VMEM)] * len(arrays)
    if not INTERPRET:
        arrays = [pltpu.with_memory_space_constraint(a, pltpu.VMEM) for a in arrays]
    to = [jax.ShapeDtypeStruct if INTERPRET else space for space in to or [pltpu.VMEM] * len(outs)]
    return pl.pallas_call(
        kernel,
        out_shape=[space(*out) for space, out in zip(to, outs, strict=True)],
        in_specs=specs,
        out_specs=[pl.BlockSpec(memory_space=pltpu.VMEM)] * len(outs),
        interpret=INTERPRET,
        **kwargs,
    )(*scalars, *arrays)


def sublane(shape):
    return lax.broadcasted_iota(jnp.int32, shape, len(shape) - 2)


def lane(shape):
    return lax.broadcasted_iota(jnp.int32, shape, len(shape) - 1)


def turn(v, shift, axis):
    size = v.shape[axis]
    shift %= size
    return v if shift == 0 else pltpu.roll(v, shift, axis)


def pack_y(gas, even_pairs, odd_pairs, _, rows, even_pay, odd_pay):
    first, last = ends("gx")
    even_x, even_y = is_even("gx"), is_even("gy")
    sub = sublane((8, 128))
    for c in range(6):
        line = []
        for i in range(12):
            if i < 2:
                below = jnp.where(even_x, odd_pairs[c, i], even_pairs[c, i])
                line.append(jnp.where(first, gas[c, 0], below))
                rows[c, i] = line[-1]
            elif i < 10:
                line.append(gas[c, i - 2])
            else:
                above = jnp.where(even_x, even_pairs[c, i - 10], odd_pairs[c, i - 10])
                line.append(jnp.where(last, gas[c, 7], above))
                rows[c, i - 8] = line[-1]
        for g in range(3):
            low = line[4 * g]
            high = turn(line[4 * g], 2, 0)
            for k in range(1, 4):
                here = (sub >= 2 * k) & (sub < 2 * k + 2)
                low = jnp.where(here, turn(line[4 * g + k], 2 * k, 0), low)
                high = jnp.where(here, turn(line[4 * g + k], 2 * k + 2, 0), high)
            even_pay[c, g] = jnp.where(even_y, high, low)
            odd_pay[c, g] = jnp.where(even_y, low, high)


def pack_z(gas, rows, even_pairs, odd_pairs, box, pay):
    even = is_even("gy")
    first, last = ends("gy")
    sub = sublane((8, 128))
    group = lane((16, 128)) // 8
    for c in range(6):
        ylo = [jnp.where(even, odd_pairs[c, g], even_pairs[c, g]) for g in range(3)]
        yhi = [jnp.where(even, even_pairs[c, g], odd_pairs[c, g]) for g in range(3)]
        packed = None
        for i in range(12):
            if 2 <= i < 10:
                mid = gas[c, i - 2]
            else:
                mid = rows[c, i if i < 2 else i - 8]
            g, k = i // 4, i % 4
            below = turn(ylo[g], 6 - 2 * k, 0)
            above = turn(yhi[g], -2 * k, 0)
            below = jnp.where(first, jnp.broadcast_to(mid[0:1], (8, 128)), below)
            above = jnp.where(last, jnp.broadcast_to(mid[7:8], (8, 128)), above)
            line = jnp.concatenate([mid, jnp.where(sub < 4, above, below)], axis=0)
            box[c, i] = line
            moved = turn(line, 8 * i + 2, 1)
            packed = moved if packed is None else jnp.where(group == i, moved, packed)
        pay[c] = packed


def primitives(state):
    r, m1, m2, m3, e, _ = state
    inv = 1.0 / r
    u = (m1 * inv, m2 * inv, m3 * inv)
    p = (GAMMA - 1.0) * (e - 0.5 * (m1 * u[0] + m2 * u[1] + m3 * u[2]))
    return u, p, jnp.sqrt(GAMMA * p * inv)


def along(state, prim, k):
    u, p, sound = prim
    uk = u[k]
    flux = [state[1 + k], state[1] * uk, state[2] * uk, state[3] * uk, (state[4] + p) * uk, state[5] * uk]
    flux[1 + k] = flux[1 + k] + p
    return flux, jnp.abs(uk) + sound, state


def face(lower, upper):
    speed = jnp.maximum(lower[1], upper[1])
    return [
        (fa + fb) - speed * (b - a)
        for fa, fb, a, b in zip(lower[0], upper[0], lower[2], upper[2], strict=True)
    ]


def over(part, move):
    flux, speed, state = part
    return [move(f) for f in flux], move(speed), [move(v) for v in state]


def advanced(state, prim, total):
    burned = RATE * state[5] * jnp.exp(-ACTIVATION * state[0] / prim[1])
    out = [v - (0.5 * TIME_STEP) * t for v, t in zip(state, total, strict=True)]
    out[4] = out[4] + (TIME_STEP * HEAT) * burned
    out[5] = out[5] - TIME_STEP * burned
    return out


def cyclic_net(state, prim, k, distance, axis):
    part = along(state, prim, k)
    faces = face(part, over(part, lambda v: turn(v, -distance, axis)))
    return faces, [f - turn(f, distance, axis) for f in faces]


def side_state(own, below, above, first, last):
    at = lane((16, 128)) % 8
    low = jnp.where(at < 2, jnp.where(first, jnp.where(at == 0, turn(own, -2, 1), turn(own, -1, 1)), below), own)
    high = jnp.where(at < 2, own, jnp.where(last, jnp.where(at == 2, turn(own, 1, 1), turn(own, 2, 1)), above))
    return jnp.where(at < 4, low, turn(high, 4, 1))


def side_inflow(faces):
    at = lane((16, 128)) % 8
    return [jnp.where(at == 0, turn(f, -5, 1), -f) for f in faces]


def closed_net(part):
    faces = face(part, over(part, lambda v: turn(v, -1, 1)))
    faces = [jnp.where(lane(f.shape) == 127, 0.0, f) for f in faces]
    return [f - turn(f, 1, 1) for f in faces]


def outer(inflow, i):
    at = lane(inflow.shape)
    return jnp.where((at == 0) | (at == 127), turn(inflow, 127 - 8 * i, 1), 0.0)


def clamp_y(v):
    first, last = ends("gy")
    sub = sublane(v.shape)
    v = jnp.where(first & (sub == 15), jnp.broadcast_to(v[0:1], v.shape), v)
    return jnp.where(last & (sub == 8), jnp.broadcast_to(v[7:8], v.shape), v)


def stage_one(box, ahead):
    state = [box[c, 0] for c in range(6)]
    part = along(state, primitives(state), 0)
    state = [box[c, 1] for c in range(6)]
    prim = primitives(state)
    next_part = along(state, prim, 0)
    faces = face(part, next_part)
    for i in range(1, 11):
        part = next_part
        next_state = [box[c, i + 1] for c in range(6)]
        next_prim = primitives(next_state)
        next_part = along(next_state, next_prim, 0)
        next_faces = face(part, next_part)
        _, net_y = cyclic_net(state, prim, 1, 1, 0)
        net_z = closed_net(along(state, prim, 2))
        total = [b - a + y + z for a, b, y, z in zip(faces, next_faces, net_y, net_z, strict=True)]
        for c, v in enumerate(advanced(state, prim, total)):
            ahead[c, i] = v
        state, prim, faces = next_state, next_prim, next_faces


def sides(own, even_pairs, odd_pairs):
    first_x, last_x = ends("gx")
    first_z, last_z = ends("gz")
    at = lane((16, 128)) % 8
    group = lane((16, 128)) // 8

    def clamp_x_z(v):
        v = jnp.where(first_x & (group == 1), turn(v, -8, 1), v)
        v = jnp.where(last_x & (group == 10), turn(v, 8, 1), v)
        v = jnp.where(first_z & (at == 1), turn(v, -1, 1), v)
        return jnp.where(last_z & (at == 6), turn(v, 1, 1), v)

    even = is_even("gz")
    side = []
    for c in range(6):
        below = jnp.where(even, odd_pairs[c], even_pairs[c])
        above = jnp.where(even, even_pairs[c], odd_pairs[c])
        side.append(side_state(own[c], below, above, first_z, last_z))
    prim = primitives(side)
    faces, net_z = cyclic_net(side, prim, 2, 1, 1)
    one = side_inflow(faces)
    _, net_x = cyclic_net(side, prim, 0, 8, 1)
    _, net_y = cyclic_net(side, prim, 1, 1, 0)
    side = advanced(side, prim, [x + y + z for x, y, z in zip(net_x, net_y, net_z, strict=True)])
    side = [clamp_y(clamp_x_z(v)) for v in side]
    return one, side_inflow(cyclic_net(side, primitives(side), 2, 1, 1)[0])


def stage_two(box, ahead, one, two, stepped, fields):
    first_x, last_x = ends("gx")

    def line(i):
        out = []
        for c in range(6):
            out.append(clamp_y(ahead[c, i] - (0.5 * TIME_STEP) * outer(one[c], i)))
        return out

    def row(i):
        v = line(i)
        if i == 1:
            v = [jnp.where(first_x, b, a) for a, b in zip(v, line(2), strict=True)]
        if i == 10:
            v = [jnp.where(last_x, b, a) for a, b in zip(v, line(9), strict=True)]
        return v

    def inner(values):
        return [v[:8] for v in values]

    def inner_prim(prim):
        return inner(prim[0]), prim[1][:8], prim[2][:8]

    state = inner(row(1))
    part = along(state, primitives(state), 0)
    full = row(2)
    full_prim = primitives(full)
    state, prim = inner(full), inner_prim(full_prim)
    next_part = along(state, prim, 0)
    faces = face(part, next_part)
    for i in range(2, 10):
        part = next_part
        next_full = row(i + 1)
        next_full_prim = primitives(next_full)
        next_state, next_prim = inner(next_full), inner_prim(next_full_prim)
        next_part = along(next_state, next_prim, 0)
        next_faces = face(part, next_part)
        _, net_y = cyclic_net(full, full_prim, 1, 1, 0)
        net_z = closed_net(along(state, prim, 2))
        total = [
            b - a + y[:8] + z + outer(s[:8], i)
            for a, b, y, z, s in zip(faces, next_faces, net_y, net_z, two, strict=True)
        ]
        x = i - 2
        done = [0.5 * box[c, i, 0:8] + 0.5 * v for c, v in enumerate(advanced(state, prim, total))]
        for c in range(6):
            stepped[c, x] = done[c]
        inv = 1.0 / done[0]
        g = [done[1 + k] * inv for k in range(3)]
        t = (GAMMA - 1.0) * (done[4] - 0.5 * (done[1] * g[0] + done[2] * g[1] + done[3] * g[2])) * inv
        for f, v in enumerate((*g, t, done[5] * inv)):
            fields[f, pl.ds(8 * (x % 4), 8), pl.ds(128 * (x // 4), 128)] = v
        full, full_prim, state, prim, faces = next_full, next_full_prim, next_state, next_prim, next_faces


def two_parts(v):
    big = v.astype(BF16)
    return big, (v - big.astype(F32)).astype(BF16)


def split_cell(cells):
    return (cells >> 7) & 31, ((cells >> 12) << 7) | (cells & 127)


def one_hot(index, count):
    return jnp.where(sublane((count, index.shape[-1])) == index, 1.0, 0.0).astype(BF16)


def numbers(info):
    return info[0, 0], info[1, 0], info[2, 0]


def in_order(order, counts, parcels, cells, sorted_parcels, sorted_cells, info):
    kept, forward, backward = counts[0, 0], counts[0, 1], counts[0, 2]
    moves, total = forward + backward, kept + forward + backward
    for k, number in enumerate((kept, forward, backward)):
        info[k : k + 1, :] = jnp.full((1, 128), number)
    info[3:8, :] = jnp.zeros((5, 128), jnp.int32)
    for j in range(64):
        b = order[0, jnp.where(j < moves, kept + j, jnp.where(j < total, j - moves, j))]
        sorted_cells[j : j + 1, :] = cells[pl.ds(b, 1), :]
        for k in range(5):
            sorted_parcels[k, j : j + 1, :] = parcels[k, pl.ds(b, 1), :]


def gather(table, cells, carried, begin, end):
    def chunk(n, _):
        start = pl.multiple_of(8 * n, 8)
        index = cells[pl.ds(start, 8), :]
        values = [[] for _ in range(5)]
        for b in range(0, 8, 2):
            pair = jnp.concatenate([index[b : b + 1], index[b + 1 : b + 2]], axis=1)
            row, column = split_cell(pair)
            found = jnp.dot(table[...], one_hot(column, 256), preferred_element_type=F32)
            chosen = sublane((32, 256)) == row
            for f in range(5):
                both = found[32 * f : 32 * f + 32] + found[160 + 32 * f : 192 + 32 * f]
                value = jnp.sum(jnp.where(chosen, both, 0.0), axis=0, keepdims=True)
                values[f] += [value[:, :128], value[:, 128:]]
        for f in range(5):
            carried[f, pl.ds(start, 8), :] = jnp.concatenate(values[f], axis=0)
        return 0

    lax.fori_loop(begin, end, chunk, 0)


def parcel_update(carried, parcels, rows):
    g = tuple(carried[k, :rows] for k in range(3))
    t, y = carried[3, :rows], carried[4, :rows]
    v = tuple(parcels[k, :rows] for k in range(3))
    mass, heat = parcels[3, :rows], parcels[4, :rows]
    root = jnp.sqrt(mass)
    inv_root = 1.0 / root
    new_mass = mass * jnp.exp((-TIME_STEP * EVAP_RATE) * t / (root * (1.0 + y * y)))
    slow = jnp.exp((-TIME_STEP / DRAG_RELAX_TIME) * inv_root)
    new_v = tuple(gk + (vk - gk) * slow for gk, vk in zip(g, v, strict=True))
    new_heat = t + (heat - t) * jnp.exp((-TIME_STEP / HEATING_RELAX) * inv_root)
    return (*v, mass, heat), (*new_v, new_mass, new_heat)


def parcel_sources(old, new):
    mass, new_mass = old[3], new[3]
    square = old[0] * old[0] + old[1] * old[1] + old[2] * old[2]
    new_square = new[0] * new[0] + new[1] * new[1] + new[2] * new[2]
    gain = [mass - new_mass]
    gain += [mass * old[k] - new_mass * new[k] for k in range(3)]
    gain += [0.5 * (mass * square - new_mass * new_square) + LIQUID_HEAT * (mass * old[4] - new_mass * new[4])]
    return gain


def gas_and_moving(
    info, box, ahead, own, even_pairs, odd_pairs, parcels, cells,
    stepped, table, carried, even_pay, odd_pay, fields, updated,
):
    _, forward, backward = numbers(info)
    one, two = sides(own, even_pairs, odd_pairs)
    stage_two(box, ahead, one, two, stepped, fields)
    for f in range(5):
        big, small = two_parts(fields[f])
        table[pl.ds(32 * f, 32), :] = big
        table[pl.ds(160 + 32 * f, 32), :] = small
    gather(table, cells, carried, 0, (forward + backward + 7) // 8)
    for k, value in enumerate(parcel_update(carried, parcels, 32)[1]):
        updated[k, 0:32] = value
        updated[k, 32:48] = jnp.zeros((16, 128), F32)

    even = is_even("gx")
    for out, up in ((even_pay, even), (odd_pay, jnp.logical_not(even))):
        start = jnp.where(up, 0, forward)
        for k in range(5):
            out[k] = updated[k, pl.ds(start, 16), :]
        out[5] = jnp.full((16, 128), jnp.where(up, forward, backward).astype(F32))


def kept_and_sources(info, stepped, table, early, parcels, cells, gas_out, updated, carried, sources, total):
    kept, forward, backward = numbers(info)
    moves = forward + backward
    chunks = (kept + moves + 7) // 8
    carried[:, 0:32] = early[...]
    gather(table, cells, carried, (moves + 7) // 8, chunks)
    old, new = parcel_update(carried, parcels, 64)
    live = sublane((64, 128)) < kept + moves
    for k, value in enumerate(parcel_sources(old, new)):
        sources[k] = jnp.where(live, value, 0.0)
        updated[k] = new[k]
    total[...] = jnp.zeros(total.shape, F32)

    def chunk(n, _):
        start = pl.multiple_of(8 * n, 8)
        index = cells[pl.ds(start, 8), :]
        given = [two_parts(sources[k, pl.ds(start, 8), :]) for k in range(5)]
        given = [[part.astype(F32) for part in parts] for parts in given]
        columns, wide = [], []
        for b in range(8):
            row, column = split_cell(index[b : b + 1, :])
            columns.append(one_hot(column, 256))
            chosen = sublane((32, 128)) == row
            wide.append(
                jnp.concatenate(
                    [
                        jnp.where(chosen, jnp.broadcast_to(given[k][half][b : b + 1, :], (32, 128)), 0.0).astype(BF16)
                        for half in range(2)
                        for k in range(5)
                    ],
                    axis=0,
                )
            )
        total[...] += lax.dot_general(
            jnp.concatenate(wide, axis=1),
            jnp.concatenate(columns, axis=1),
            (((1,), (1,)), ((), ())),
            preferred_element_type=F32,
        )
        return 0

    lax.fori_loop(0, chunks, chunk, 0)
    for c in range(6):
        k = c % 5
        both = total[32 * k : 32 * k + 32] + total[160 + 32 * k : 192 + 32 * k]
        for half in range(2):
            added = jnp.reshape(both[:, 128 * half : 128 * half + 128], (4, 8, 128))
            gas_out[c, 4 * half : 4 * half + 4] = stepped[c, 4 * half : 4 * half + 4] + added


def place(info, updated, even_pairs, odd_pairs, gas, moved, gas_out):
    kept, forward, backward = numbers(info)
    moves = forward + backward
    gas_out[...] = gas[...]
    first, last = ends("gx")
    even = is_even("gx")
    from_lower = jnp.where(first, 0.0, jnp.where(even, odd_pairs[5, 0, 0], even_pairs[5, 0, 0])).astype(jnp.int32)
    from_upper = jnp.where(last, 0.0, jnp.where(even, even_pairs[5, 0, 0], odd_pairs[5, 0, 0])).astype(jnp.int32)
    slot = sublane((32, 128))
    near = sublane((16, 128))
    for k in range(5):
        moved[k, 0:32] = jnp.where(slot < kept, updated[k, pl.ds(moves, 32), :], 0.0)
        moved[k, 32:64] = jnp.zeros((32, 128), F32)
    for k in range(5):
        lower = jnp.where(even, odd_pairs[k], even_pairs[k])
        moved[k, pl.ds(kept, 16), :] = jnp.where(near < from_lower, lower, 0.0)
    for k in range(5):
        upper = jnp.where(even, even_pairs[k], odd_pairs[k])
        moved[k, pl.ds(kept + from_lower, 16), :] = jnp.where(near < from_upper, upper, 0.0)


def body(gas, parcels, home_cell_index, order, counts):
    even = is_even("gx")
    edges = [
        lax.dynamic_slice_in_dim(gas, jnp.where(even, near, far), 2, 1) for near, far in ((6, 0), (0, 6))
    ]
    x_halo = swapped(edges, "gx")
    sorted_parcels, cells, info = call(
        in_order,
        [(5, 64, 128), ((64, 128), jnp.int32), ((8, 128), jnp.int32)],
        [order, counts],
        [jnp.transpose(parcels, (1, 0, 2)), home_cell_index],
    )
    rows, *pays = call(pack_y, [(6, 4, 8, 128), (6, 3, 8, 128), (6, 3, 8, 128)], [], [gas, *x_halo, cells])
    y_halo = swapped(pays, "gy")
    box, pay = call(pack_z, [(6, 12, 16, 128), (6, 16, 128)], [], [gas, rows, *y_halo])
    z_halo = swapped([pay, pay], "gz")
    (ahead,) = call(stage_one, [(6, 12, 16, 128)], [], [box])
    stepped, table, carried, *pays = call(
        gas_and_moving,
        [(6, 8, 8, 128), ((320, 256), BF16), (5, 32, 128), (6, 16, 128), (6, 16, 128)],
        [],
        [info, box, ahead, pay, *z_halo, sorted_parcels, cells],
        scratch_shapes=[pltpu.VMEM((5, 32, 256), F32), pltpu.VMEM((5, 48, 128), F32)],
    )
    arrived = swapped(pays, "gx")
    gas_done, updated = call(
        kept_and_sources,
        [(6, 8, 8, 128), (5, 64, 128)],
        [],
        [info, stepped, table, carried, sorted_parcels, cells],
        scratch_shapes=[
            pltpu.VMEM((5, 64, 128), F32),
            pltpu.VMEM((5, 64, 128), F32),
            pltpu.VMEM((320, 256), F32),
        ],
    )
    moved, gas_out = call(
        place, [(5, 64, 128), (6, 8, 8, 128)], [], [info, updated, *arrived, gas_done], to=[pltpu.HBM] * 2
    )
    return gas_out, jnp.transpose(moved, (1, 0, 2))


def solution(mesh):
    blocks = ("gx", "gy", "gz")
    in_specs = (
        P(None, *blocks),
        P(blocks, None, None),
        P(blocks, None),
        P(blocks, None),
        P(blocks, None),
    )
    out_specs = (P(None, *blocks), P(blocks, None, None))
    return jax.shard_map(body, mesh=mesh, in_specs=in_specs, out_specs=out_specs, check_vma=False)
```
